32 devices in a mesh: slab: 2 (over y), docs: 4 (over x, core), blk: 4 (over z).
Axes of the slice: x: 2, y: 2, z: 4, core: 2. Of those that a mesh axis runs over, the one named last changes fastest.
Arguments:
- pooled: bfloat16 [16384, 768], P(('slab', 'docs', 'blk')), parts along dimension 0, may hold values from -6 to 6
- proj_weight: bfloat16 [768, 768], replicated, may hold values from -0.21875 to 0.21875
- cluster: int32 [16384], P(('slab', 'docs', 'blk')), parts along dimension 0, may hold values from 0 to 143, as said below
Outputs:
- best_sim: float32 [16384], P(('slab', 'docs', 'blk')), parts along dimension 0
The draws below stay inside these ranges and needn't reach their ends.
There are 2 independent parts, one for each index of `slab`. The reference program is written for one: setup_inputs(seed, part) draws one part's arguments, and reference() takes and returns one part's arrays. A program takes and returns all parts, laid end to end along the dimension named above; an argument that names none is the same for every part. Nothing has to cross between parts.
Inputs may be any that keep to these rules, and one draw needn't show every extreme that they name: Clusters below 16 are large, the others small. The documents of one device hold exactly 128 of large clusters and 384 of small ones. Among one device's documents at most 64 of large clusters share the value of cluster modulo the size of docs, and at most 48 of small clusters share the value of (cluster - 16) modulo the number of devices of docs and blk; in every draw one value of each kind holds exactly that many on every device.
All inputs are finite; a program needn't handle non-finite values.
Results may differ from the reference program's by a relative error of at most 0.0012.
Values may be sent and summed in bfloat16 or wider, within the bound.
A program may use at most 64 MiB of HBM per device.

```python
import jax
import jax.numpy as jnp
from jax import lax

D = 768
BIG_OWN = 4
SMALL_OWN = 8
BIG_DEV = 128
SMALL_DEV = 384
LARGE_CL = 16
CAPB = 64
CAPS = 48
DOCS = 8192
N_DOCS = 4
N_BLK = 4


def draw_cluster(key, part):
    devices = N_DOCS * N_BLK
    hot_owner = jax.random.randint(jax.random.fold_in(key, 11), (), 0, N_DOCS).astype(jnp.int32)
    hot_target = jax.random.randint(jax.random.fold_in(key, 12), (), 0, devices).astype(jnp.int32)
    device_keys = jax.random.split(jax.random.fold_in(key, 13), devices)

    def one_device(device_key):
        subkeys = jax.random.split(device_key, 7)
        big_slots = N_DOCS * CAPB
        big_owner = jnp.arange(big_slots, dtype=jnp.int32) // CAPB
        big_pri = jnp.where(big_owner == hot_owner, 0, 1) * big_slots + jax.random.permutation(subkeys[0], big_slots).astype(jnp.int32)
        chosen = jnp.argsort(big_pri)[:BIG_DEV]
        owners = big_owner[chosen]
        big_rank = jnp.minimum(jax.random.randint(subkeys[1], (BIG_DEV,), 0, BIG_OWN), jax.random.randint(subkeys[2], (BIG_DEV,), 0, BIG_OWN))
        big_ids = owners + N_DOCS * big_rank
        small_slots = devices * CAPS
        small_target = jnp.arange(small_slots, dtype=jnp.int32) // CAPS
        small_pri = jnp.where(small_target == hot_target, 0, 1) * small_slots + jax.random.permutation(subkeys[3], small_slots).astype(jnp.int32)
        picked = jnp.argsort(small_pri)[:SMALL_DEV]
        targets = small_target[picked]
        small_rank = jnp.minimum(jax.random.randint(subkeys[4], (SMALL_DEV,), 0, SMALL_OWN), jax.random.randint(subkeys[5], (SMALL_DEV,), 0, SMALL_OWN))
        small_ids = LARGE_CL + targets + devices * small_rank
        all_ids = jnp.concatenate([big_ids, small_ids]).astype(jnp.int32)
        return jax.random.permutation(subkeys[6], all_ids)
    return jax.vmap(one_device)(device_keys).reshape(-1).astype(jnp.int32)


def block_scale(own_key, shape, cuts, smallest, top_value):
    level, own = 1.0, jax.random.fold_in(own_key, 6)
    for axis_at, shards_of in cuts:
        steps = jnp.exp(jax.random.uniform(jax.random.fold_in(own, axis_at), (shards_of,), jnp.float32, smallest / len(cuts), top_value / len(cuts)))
        level = level * jnp.repeat(steps, shape[axis_at] // shards_of).reshape([-1 if axis == axis_at else 1 for axis in range(len(shape))])
    return level


def bell_draw(stream_key, shape, width, reach, shards=(), held_as=jnp.bfloat16):
    drawn = jax.random.normal(stream_key, shape, jnp.float32) * width
    if len(shards) > 0:
        drawn = block_scale(stream_key, shape, shards, -0.22, 0.18) * drawn
    return jnp.clip(drawn, min=-reach, max=reach).astype(held_as)


def setup_inputs(seed: int = 0, part: int = 0) -> dict:
    arg_keys = jax.random.split(jax.random.key(seed), 4)
    part_splits = jax.random.split(jax.random.fold_in(arg_keys[3], part), 4)
    return {
        "pooled": bell_draw(part_splits[0], (DOCS, D), 1.0, 6.0, ((0, 16),)),
        "proj_weight": bell_draw(arg_keys[1], (D, D), D ** -0.5, 0.21875),
        "cluster": draw_cluster(jax.random.fold_in(jax.random.fold_in(arg_keys[3], part), 71), part),
    }


def group_best(embedded, cluster, group_of, groups, capacity):
    total_rows = embedded.shape[0]
    feature = embedded.shape[1]
    positions = jnp.arange(total_rows, dtype=jnp.int32)
    group_key = jnp.where(group_of >= 0, group_of, groups).astype(jnp.int32)
    sort_order = jnp.argsort(group_key * total_rows + positions).astype(jnp.int32)
    sorted_key = group_key[sort_order]
    group_sizes = jax.ops.segment_sum(jnp.ones((total_rows,), jnp.int32), group_key, num_segments=groups + 1)
    starts = (jnp.cumsum(group_sizes) - group_sizes).astype(jnp.int32)
    sorted_rank = positions - starts[sorted_key]
    slot_rank = jnp.zeros((total_rows,), jnp.int32).at[sort_order].set(sorted_rank)
    slot = jnp.where(group_of >= 0, group_key * capacity + slot_rank, groups * capacity).astype(jnp.int32)
    padded = jnp.zeros((groups * capacity, feature), embedded.dtype).at[slot].set(embedded, mode='drop')
    padded_ids = jnp.full((groups * capacity,), -1, jnp.int32).at[slot].set(cluster, mode='drop')
    padded = padded.reshape(groups, capacity, feature)
    padded_ids = padded_ids.reshape(groups, capacity)

    def group_scan(operands):
        block_rows, block_ids = operands
        scores = jnp.dot(block_rows, block_rows.T, preferred_element_type=jnp.float32)
        inside = jnp.arange(capacity, dtype=jnp.int32)
        allowed = (block_ids[:, None] == block_ids[None, :]) & (block_ids[:, None] >= 0) & (inside[:, None] != inside[None, :])
        return lax.optimization_barrier(jnp.max(jnp.where(allowed, scores, -1.0), axis=1))
    best_all = lax.map(group_scan, (padded, padded_ids)).reshape(-1)
    return best_all[jnp.minimum(slot, groups * capacity - 1)]

def reference(pooled, proj_weight, cluster):
    projected = jnp.dot(pooled, proj_weight, preferred_element_type=jnp.float32)
    embedded = (projected / jnp.sqrt(lax.optimization_barrier(jnp.sum(projected * projected, axis=1, keepdims=True)) + 1e-06)).astype(jnp.bfloat16)
    is_big = cluster < LARGE_CL
    big_group = jnp.where(is_big, cluster % N_DOCS, -1).astype(jnp.int32)
    small_group = jnp.where(is_big, -1, (cluster - LARGE_CL) % (N_DOCS * N_BLK)).astype(jnp.int32)
    best_big = group_best(embedded, cluster, big_group, N_DOCS, N_DOCS * N_BLK * CAPB)
    best_small = group_best(embedded, cluster, small_group, N_DOCS * N_BLK, N_DOCS * N_BLK * CAPS)
    return jnp.where(is_big, best_big, best_small)
```

```python
import functools

import jax
import jax.numpy as jnp
from jax import lax
from jax.experimental import pallas as pl
from jax.experimental.pallas import tpu as pltpu
from jax.sharding import PartitionSpec as P

MESH = pl.DeviceIdType.MESH
BIG_OWN = 4
LANES = 128
F32 = jnp.float32
BF16 = jnp.bfloat16


def up(value, step):
    return -(-value // step) * step


def iota(shape, dim):
    return lax.broadcasted_iota(jnp.int32, shape, dim)


def nt(a, b):
    return lax.dot_general(a, b, (((1,), (1,)), ((), ())), preferred_element_type=F32)


def exact_dot(a, b):
    high = a.astype(BF16)
    rest = a - high.astype(F32)
    middle = rest.astype(BF16)
    low = (rest - middle.astype(F32)).astype(BF16)
    three = jnp.dot(jnp.concatenate([high, middle, low], axis=0), b.astype(BF16), preferred_element_type=F32)
    m = a.shape[0]
    return three[:m] + three[m : 2 * m] + three[2 * m :]


def kernel(
    dims, pooled_hbm, weight_hbm, cluster_ref, out_ref, flag_ref,
    pooled, weight, embedded, small_send, relay, small_recv, big_send, big_all, small_over, big_over,
    ids_send, ids_recv, flags, big_marks, back_send, back_recv,
    in_sem, ids_ss, ids_rs, side_ss, side_rs, small_ss, small_rs, one_ss, one_rs, two_ss, two_rs,
    sback_ss, sback_rs, bback_ss, bback_rs, sover_ss, sover_rs, over_ss, over_rs, bover_ss, bover_rs, flag_ss, flag_rs,
):
    slabs, shards, blocks, cs, ms, cb, mb = dims
    tight = ms < cs
    n = shards * blocks
    rows = pooled.shape[0]
    nb = back_recv.shape[0]
    limit = BIG_OWN * shards
    cores = 2 if shards % 2 == 0 else 1
    chips = shards // cores
    half = blocks // 2
    me_s, me_d, me_b = lax.axis_index("slab"), lax.axis_index("docs"), lax.axis_index("blk")
    me_x, me_c = me_d // cores, lax.rem(me_d, cores)
    group = blocks * cb
    far = [j for j in range(blocks) if j & half]
    near = [j for j in range(1, blocks) if not j & half]
    away = far + near

    def docs_at(r, sign=1):
        dx, dc = r // cores, r % cores
        return lax.rem(me_x + sign * dx + chips, chips) * cores + lax.rem(me_c + dc, cores)

    def blk_at(j):
        return me_b ^ j

    peers = [(r * blocks + j, r, j) for j in away + [0] for r in range(shards - 1, -1, -1) if (r, j) != (0, 0)]

    load_rows = pltpu.make_async_copy(pooled_hbm, pooled, in_sem.at[0])
    load_weight = pltpu.make_async_copy(weight_hbm, weight, in_sem.at[1])
    load_rows.start()
    load_weight.start()
    barrier = pltpu.get_barrier_semaphore()
    for _, r, j in peers:
        pl.semaphore_signal(
            barrier, inc=1, device_id={"docs": docs_at(r), "blk": blk_at(j)}, device_id_type=MESH
        )
    others = range(1, slabs) if tight else ()
    for s in others:
        pl.semaphore_signal(barrier, inc=1, device_id={"slab": lax.rem(me_s + s, slabs)}, device_id_type=MESH)

    def copy(src, dst, ssem, rsem, d, b):
        return pltpu.make_async_remote_copy(
            src_ref=src, dst_ref=dst, send_sem=ssem, recv_sem=rsem,
            device_id={"docs": d, "blk": b}, device_id_type=MESH,
        )

    def chunk(ref, index, size, count=None):
        return ref.at[pl.ds(index * size, size if count is None else count)]

    def extra(ref, index, size, skip):
        return ref.at[pl.ds(index * size + skip, size - skip)]

    def ids_copy(q, r, j):
        return copy(ids_send.at[q], ids_recv.at[q], ids_ss.at[q], ids_rs.at[q], docs_at(r), blk_at(j))

    def side_copy(r, j):
        q = r * blocks + j
        into = relay if j else small_recv
        count = ms if j in far else cs
        return copy(
            chunk(small_send, q, cs, count), chunk(into, q, cs, count), side_ss.at[q], side_rs.at[q], docs_at(r), me_b
        )

    def line_copy(r, j):
        q = r * blocks + j
        count = ms if j in far else cs
        return copy(
            chunk(relay, q, cs, count), chunk(small_recv, q, cs, count), small_ss.at[q], small_rs.at[q], me_d, blk_at(j)
        )

    def one_copy(j):
        count = mb if j in far else cb
        return copy(
            chunk(big_send, j, cb, count), chunk(big_all, j, cb, count), one_ss.at[j], one_rs.at[j], me_d, blk_at(j)
        )

    def two_copy(r):
        if r == 1 or r % cores == 0:
            return copy(chunk(big_all, 0, group), chunk(big_all, r, group), two_ss.at[r], two_rs.at[r], docs_at(r), me_b)
        return copy(
            chunk(big_all, r - 1, group), chunk(big_all, r, group), two_ss.at[r], two_rs.at[r], docs_at(1), me_b
        )

    def sover_copy(j, i):
        src = small_over.at[:] if i is None else extra(small_recv, i, cs, ms)
        return copy(
            src, extra(small_recv, j, cs, ms), sover_ss.at[j], sover_rs.at[j], me_d, blk_at(half if i is None else i ^ j)
        )

    def bover_copy(j, i):
        src = big_over.at[:] if i is None else extra(big_all, i, cb, mb)
        return copy(
            src, extra(big_all, j, cb, mb), bover_ss.at[j], bover_rs.at[j], me_d, blk_at(half if i is None else i ^ j)
        )

    def over_copy(r, j):
        q = r * blocks + j
        return copy(
            extra(small_recv, j, cs, ms), extra(small_recv, q, cs, ms), over_ss.at[q], over_rs.at[q], docs_at(r), me_b
        )

    def flag_copy(s):
        return pltpu.make_async_remote_copy(
            src_ref=flags.at[0], dst_ref=flags.at[s], send_sem=flag_ss.at[s], recv_sem=flag_rs.at[s],
            device_id={"slab": lax.rem(me_s + s, slabs)}, device_id_type=MESH,
        )

    hops = []
    held = [half]
    bit = 1
    while bit < half:
        hops += [(j ^ bit, j) for j in held]
        held = held + [j ^ bit for j in held]
        bit *= 2

    def sback_copy(q, r, j):
        return copy(
            back_send.at[q], back_recv.at[q], sback_ss.at[q], sback_rs.at[q], docs_at(r, -1), blk_at(j)
        )

    def bback_copy(j):
        return copy(back_send.at[n + j], back_recv.at[n + j], bback_ss.at[j], bback_rs.at[j], me_d, blk_at(j))

    cluster = cluster_ref[...]
    is_big = cluster < limit
    rest = jnp.maximum(cluster - limit, 0)
    level = rest // n
    owner = lax.rem(rest + 2 * level, n) if tight else lax.rem(rest, n)
    owner_b, owner_d = owner // shards, lax.rem(owner, shards)
    side = lax.rem(owner_d // cores - me_x + chips, chips) * cores + lax.rem(lax.rem(owner_d, cores) - me_c + cores, cores)
    line = owner_b ^ me_b
    big_level = cluster // blocks
    turn = lax.rem(big_level, blocks)
    turn = lax.rem(turn, 2) * half + turn // 2 if tight else 0 * turn
    big_line = lax.rem(lax.rem(cluster, blocks) + turn, blocks) ^ me_b
    bucket = jnp.where(is_big, n + big_line, side * blocks + line)
    local_id = jnp.where(is_big, big_level, level) + 1
    onehot = iota((nb, rows), 0) == bucket
    upper = (iota((rows, rows), 0) < iota((rows, rows), 1)).astype(BF16)
    before = jnp.dot(onehot.astype(BF16), upper, preferred_element_type=F32)
    rank = jnp.sum(jnp.where(onehot, before, 0.0), axis=0, keepdims=True).astype(jnp.int32)
    if tight:
        main = jnp.where(is_big, mb, ms)
        is_far = jnp.where(is_big, big_line, line) >= half
        over = is_far & (rank >= main)
        kinds = jnp.where(over, jnp.where(is_big, 1, 0), -1)
        which = iota((16, rows), 0) == kinds
        before = jnp.dot(which.astype(BF16), upper, preferred_element_type=F32)
        extra_rank = jnp.sum(jnp.where(which, before, 0.0), axis=0, keepdims=True).astype(jnp.int32)
        place = jnp.where(over, main + extra_rank, rank)
        lost = over & (place >= jnp.where(is_big, cb, cs))
        flag = jnp.max(jnp.where(lost, 1.0, 0.0), axis=1, keepdims=True)
    else:
        over = None
        place = rank
    at_place = iota((LANES, rows), 0) == place
    ids = nt(jnp.where(onehot, local_id.astype(F32), 0.0).astype(BF16), at_place.astype(BF16))
    if tight:
        ids = jnp.where(iota((nb, LANES), 1) == LANES - 1, flag, ids)
    for q in range(n):
        g = n + q % blocks
        ids_send[q] = jnp.concatenate([ids[q : q + 1], ids[g : g + 1]], axis=1)
    ids_recv[0] = ids_send[0]
    for q in range(n + blocks, nb):
        back_recv[q] = jnp.zeros((1, LANES), F32)

    load_rows.wait()
    load_weight.wait()
    projected = jnp.dot(pooled[...], weight[...], preferred_element_type=F32)
    norm = jnp.sqrt(jnp.sum(projected * projected, axis=1, keepdims=True) + 1e-06)
    embedded[...] = (projected / norm).astype(BF16)

    def pick(slot, base, count):
        chosen = (iota((count, rows), 0) + base == slot).astype(BF16)
        return jnp.dot(chosen, embedded[...], preferred_element_type=F32).astype(BF16)

    if tight:
        small_over[...] = pick(jnp.where(over & ~is_big, place, -1), ms, cs - ms)
        big_over[...] = pick(jnp.where(over & is_big, place, -1), mb, cb - mb)
        kept = ~over
    else:
        kept = place >= 0
    big_slot = jnp.where(is_big & kept, (bucket - n) * cb + place, -1)
    big_send[...] = pick(big_slot, 0, group)

    big_all[0:cb, :] = big_send[0:cb, :]

    small_slot = jnp.where(is_big | ~kept, -1, bucket * cs + place)
    order = [r for r in range(cores, shards)] + [r for r in range(1, cores)] + [0]
    span = blocks * cs
    for r in order:
        picked = pick(small_slot, r * span, span)
        if r:
            small_send[r * span : (r + 1) * span, :] = picked
        else:
            relay[0:span, :] = picked
            small_recv[0:cs, :] = picked[0:cs]

    pl.semaphore_wait(barrier, n - 1 + len(others))
    if tight:
        bover_copy(half, None).start()
        sover_copy(half, None).start()
    for j in far:
        one_copy(j).start()
    for j in far:
        for r in order:
            (side_copy if r else line_copy)(r, j).start()
    for j in near:
        one_copy(j).start()
    for j in near:
        for r in order:
            (side_copy if r else line_copy)(r, j).start()
    for q, r, j in peers:
        ids_copy(q, r, j).start()
    for r in order:
        if r:
            side_copy(r, 0).start()

    if tight:
        for j, i in [(half, None)] + hops:
            bover_copy(j, i).wait_recv()
            for j2, i2 in hops:
                if i2 == j:
                    bover_copy(j2, i2).start()
            sover_copy(j, i).wait_recv()
            for j2, i2 in hops:
                if i2 == j:
                    sover_copy(j2, i2).start()
            for r in order:
                if r:
                    over_copy(r, j).start()

    passed = [(r, j) for r in range(1, shards) for j in away]
    for r in range(1, shards):
        if r == cores:
            for j in away:
                one_copy(j).wait_recv()
            for r2 in range(1, shards):
                if r2 == 1 or r2 % cores == 0:
                    two_copy(r2).start()
        for j in away:
            side_copy(r, j).wait_recv()
            line_copy(r, j).start()

    for q, r, j in peers:
        ids_copy(q, r, j).wait_recv()
    if tight:
        seen = jnp.max(ids_recv[:, 0, 0:LANES], axis=0, keepdims=True)
        flags[0] = seen
        for s in others:
            flag_copy(s).start()
    total = n * cs
    low = iota((total, n), 1) * cs
    at = iota((total, n), 0)
    inside = (at >= low) & (at < low + cs)
    base = jnp.sum(jnp.where(inside, low, 0).astype(F32), axis=1, keepdims=True).astype(jnp.int32)
    small_lane = iota((total, LANES), 1) == iota((total, LANES), 0) - base
    marks = jnp.dot(inside.astype(BF16), ids_recv[:, 0, 0:LANES].astype(BF16), preferred_element_type=F32)
    marks = jnp.where(small_lane, marks, 0.0)
    small_col = jnp.sum(marks, axis=1, keepdims=True)
    small_row = nt(jnp.ones((8, LANES), BF16), marks.astype(BF16))[0:1]

    big_total = n * cb
    low = iota((big_total, n), 1) * cb
    at = iota((big_total, n), 0)
    inside = (at >= low) & (at < low + cb)
    base = jnp.sum(jnp.where(inside, low, 0).astype(F32), axis=1, keepdims=True).astype(jnp.int32)
    marks = jnp.dot(inside.astype(BF16), ids_recv[:, 0, LANES:].astype(BF16), preferred_element_type=F32)
    big_marks[...] = jnp.where(iota((big_total, LANES), 1) == iota((big_total, LANES), 0) - base, marks, 0.0)

    my_row = nt(jnp.ones((8, LANES), BF16), big_marks[0:group, :].astype(BF16))[0:1]
    best = jnp.full((1, group), -1.0, F32)
    for r in range(shards):
        if r:
            two_copy(r).wait_recv()
            if r % cores == 0 and cores > 1:
                two_copy(r + 1).start()
        theirs = pl.ds(r * group, group)
        scores = nt(big_all[theirs, :], big_all[0:group, :])
        allowed = jnp.sum(big_marks[theirs, :], axis=1, keepdims=True) == my_row
        if r == 0:
            allowed = allowed & (iota((group, group), 0) != iota((group, group), 1))
        best = jnp.maximum(best, jnp.max(jnp.where(allowed, scores, -1.0), axis=0, keepdims=True))
    low = iota((up(blocks, 16), group), 0) * cb
    at = iota((up(blocks, 16), group), 1)
    spread = jnp.where((at >= low) & (at < low + cb), best, 0.0)
    spot = lax.rem(iota((group, LANES), 0), cb) == iota((group, LANES), 1)
    back = exact_dot(spread, spot.astype(F32))
    for b in range(blocks):
        back_send[n + b] = back[b : b + 1]
    for j in away:
        bback_copy(j).start()
    back_recv[n] = back_send[n]

    def small_best(r0, r1, c0, c1):
        scores = nt(small_recv[r0:r1, :], small_recv[c0:c1, :])
        allowed = small_col[r0:r1] == small_row[:, c0:c1]
        if r0 < c1 and c0 < r1:
            allowed = allowed & (iota((r1 - r0, c1 - c0), 0) + r0 != iota((r1 - r0, c1 - c0), 1) + c0)
        return jnp.max(jnp.where(allowed, scores, -1.0), axis=0, keepdims=True)

    width = next(w for w in (256, 128, total) if total % w == 0)
    cut = total - span
    if tight:
        for r in range(1, shards):
            for j in far:
                over_copy(r, j).wait_recv()
    parts = []
    for r in range(shards):
        if r == shards - 1:
            parts = [small_best(0, cut, c, c + width) for c in range(0, cut - width + 1, width)]
        for j in range(blocks):
            if (r, j) != (0, 0):
                (line_copy if j else side_copy)(r, j).wait_recv()
    for c in range(0, total, width):
        late = small_best(cut, total, c, c + width)
        if c // width < len(parts):
            parts[c // width] = jnp.maximum(parts[c // width], late)
        else:
            parts.append(jnp.maximum(small_best(0, cut, c, c + width), late))
    best = jnp.concatenate(parts, axis=1) if len(parts) > 1 else parts[0]
    low = iota((n, total), 0) * cs
    at = iota((n, total), 1)
    spread = jnp.where((at >= low) & (at < low + cs), best, 0.0)
    back = exact_dot(spread, small_lane.astype(F32))
    for q in range(n):
        back_send[q] = back[q : q + 1]
    for q, r, j in peers:
        sback_copy(q, r, j).start()
    back_recv[0] = back_send[0]

    if tight:
        for s in others:
            flag_copy(s).wait_recv()
            flag_copy(s).wait_send()
        flag_ref[...] = jnp.max(flags[:, 0, :], axis=0, keepdims=True)
    else:
        flag_ref[...] = jnp.zeros_like(flag_ref)

    for j in away:
        bback_copy(j).wait_recv()
    for q, r, j in peers:
        sback_copy(q, r, j).wait_recv()
    result = exact_dot(back_recv[:, 0, :], at_place.astype(F32))
    out_ref[...] = jnp.sum(jnp.where(onehot, result, 0.0), axis=0, keepdims=True)

    for j in away:
        one_copy(j).wait_send()
        bback_copy(j).wait_send()
    for r in range(1, shards):
        two_copy(r).wait_send()
    for q, r, j in peers:
        ids_copy(q, r, j).wait_send()
        sback_copy(q, r, j).wait_send()
        if r:
            side_copy(r, j).wait_send()
        if j:
            line_copy(r, j).wait_send()
    if tight:
        for j, i in [(half, None)] + hops:
            bover_copy(j, i).wait_send()
            sover_copy(j, i).wait_send()
            for r in range(1, shards):
                over_copy(r, j).wait_send()


def solution(mesh):
    slabs, shards, blocks = mesh.shape["slab"], mesh.shape["docs"], mesh.shape["blk"]
    n = shards * blocks

    def body(pooled, proj_weight, cluster):
        rows, width = pooled.shape
        feature = proj_weight.shape[1]
        big_count = rows // 4
        cap_big = 2 * big_count // shards
        cap_small = 2 * (rows - big_count) // n
        cs = up(cap_small, 16)
        cb = up(cap_big * (shards // blocks), 16)
        nb = up(n + blocks, 16)
        dma = pltpu.SemaphoreType.DMA

        def call(ms, mb, collective_id):
            return pl.pallas_call(
                functools.partial(kernel, (slabs, shards, blocks, cs, ms, cb, mb)),
                out_shape=(jax.ShapeDtypeStruct((1, rows), F32), jax.ShapeDtypeStruct((1, LANES), F32)),
                in_specs=[
                    pl.BlockSpec(memory_space=pl.ANY),
                    pl.BlockSpec(memory_space=pl.ANY),
                    pl.BlockSpec(memory_space=pltpu.VMEM),
                ],
                out_specs=(pl.BlockSpec(memory_space=pltpu.VMEM), pl.BlockSpec(memory_space=pltpu.VMEM)),
                scratch_shapes=[
                    pltpu.VMEM((rows, width), BF16),
                    pltpu.VMEM((width, feature), BF16),
                    pltpu.VMEM((rows, feature), BF16),
                    pltpu.VMEM((n * cs, feature), BF16),
                    pltpu.VMEM((n * cs, feature), BF16),
                    pltpu.VMEM((n * cs, feature), BF16),
                    pltpu.VMEM((blocks * cb, feature), BF16),
                    pltpu.VMEM((n * cb, feature), BF16),
                    pltpu.VMEM((max(cs - ms, 16), feature), BF16),
                    pltpu.VMEM((max(cb - mb, 16), feature), BF16),
                    pltpu.VMEM((n, 1, 2 * LANES), F32),
                    pltpu.VMEM((n, 1, 2 * LANES), F32),
                    pltpu.VMEM((slabs, 1, LANES), F32),
                    pltpu.VMEM((n * cb, LANES), F32),
                    pltpu.VMEM((n + blocks, 1, LANES), F32),
                    pltpu.VMEM((nb, 1, LANES), F32),
                    dma((2,)), dma((n,)), dma((n,)), dma((n,)), dma((n,)), dma((n,)), dma((n,)),
                    dma((blocks,)), dma((blocks,)), dma((shards,)), dma((shards,)), dma((n,)), dma((n,)),
                    dma((blocks,)), dma((blocks,)), dma((blocks,)), dma((blocks,)), dma((n,)), dma((n,)),
                    dma((blocks,)), dma((blocks,)), dma((slabs,)), dma((slabs,)),
                ],
                compiler_params=pltpu.CompilerParams(
                    collective_id=collective_id, has_side_effects=True, vmem_limit_bytes=60 * 1024 * 1024
                ),
            )(pooled, proj_weight, cluster.reshape(1, rows))

        ms, mb = up(2 * cs // 3, 16), up(cb // 2, 16)
        if ms < cs and mb < cb:
            best, flag = call(ms, mb, 0)
            best = lax.cond(flag[0, LANES - 1] > 0.0, lambda: call(cs, cb, 1)[0], lambda: best)
        else:
            best, _ = call(cs, cb, 0)
        return jnp.maximum(best.reshape(rows), -1.0)

    in_specs = (P(("slab", "docs", "blk"), None), P(), P(("slab", "docs", "blk")))
    out_specs = P(("slab", "docs", "blk"))
    return jax.shard_map(body, mesh=mesh, in_specs=in_specs, out_specs=out_specs, check_vma=False)
```

```python
import functools

import jax
import jax.numpy as jnp
from jax import lax
from jax.experimental import pallas as pl
from jax.experimental.pallas import tpu as pltpu
from jax.sharding import PartitionSpec as P

MESH = pl.DeviceIdType.MESH
BIG_OWN = 4
LANES = 128
F32 = jnp.float32
BF16 = jnp.bfloat16


def up(value, step):
    return -(-value // step) * step


def iota(shape, dim):
    return lax.broadcasted_iota(jnp.int32, shape, dim)


def nt(a, b):
    return lax.dot_general(a, b, (((1,), (1,)), ((), ())), preferred_element_type=F32)


def exact_dot(a, b):
    high = a.astype(BF16)
    rest = a - high.astype(F32)
    middle = rest.astype(BF16)
    low = (rest - middle.astype(F32)).astype(BF16)
    three = jnp.dot(jnp.concatenate([high, middle, low], axis=0), b.astype(BF16), preferred_element_type=F32)
    m = a.shape[0]
    return three[:m] + three[m : 2 * m] + three[2 * m :]


def kernel(
    dims, pooled_hbm, weight_hbm, cluster_ref, out_ref, flag_ref,
    pooled, weight, embedded, small_send, relay, small_recv, big_send, big_all, small_over, big_over,
    ids_send, ids_recv, flags, big_marks, small_back, big_back, back_recv,
    in_sem, ids_ss, ids_rs, side_ss, side_rs, small_ss, small_rs, one_ss, one_rs, two_ss, two_rs,
    sback_ss, sback_rs, bback_ss, bback_rs, sover_ss, sover_rs, over_ss, over_rs, bover_ss, bover_rs, flag_ss, flag_rs, joined,
):
    slabs, shards, blocks, cs, ms, cb, mb = dims
    tight = ms < cs
    n = shards * blocks
    rows = pooled.shape[0]
    nb = back_recv.shape[0]
    limit = BIG_OWN * shards
    cores = 2 if shards % 2 == 0 else 1
    chips = shards // cores
    half = blocks // 2
    me_s, me_d, me_b = lax.axis_index("slab"), lax.axis_index("docs"), lax.axis_index("blk")
    me_x, me_c = me_d // cores, lax.rem(me_d, cores)
    group = blocks * cb
    far = [j for j in range(blocks) if j & half]
    near = [j for j in range(1, blocks) if not j & half]
    away = far + near

    def docs_at(r, sign=1):
        dx, dc = r // cores, r % cores
        return lax.rem(me_x + sign * dx + chips, chips) * cores + lax.rem(me_c + dc, cores)

    def blk_at(j):
        return me_b ^ j

    peers = [(r * blocks + j, r, j) for j in away + [0] for r in range(shards - 1, -1, -1) if (r, j) != (0, 0)]

    load_rows = pltpu.make_async_copy(pooled_hbm, pooled, in_sem.at[0])
    load_weight = pltpu.make_async_copy(weight_hbm, weight, in_sem.at[1])
    load_rows.start()
    load_weight.start()
    barrier = pltpu.get_barrier_semaphore()
    straight = [(r, j) for _, r, j in peers if r == 0 or j == 0]
    for r, j in straight:
        pl.semaphore_signal(
            barrier, inc=1, device_id={"docs": docs_at(r), "blk": blk_at(j)}, device_id_type=MESH
        )
    others = range(1, slabs) if tight else ()
    for s in others:
        pl.semaphore_signal(barrier, inc=1, device_id={"slab": lax.rem(me_s + s, slabs)}, device_id_type=MESH)

    def copy(src, dst, ssem, rsem, d, b):
        return pltpu.make_async_remote_copy(
            src_ref=src, dst_ref=dst, send_sem=ssem, recv_sem=rsem,
            device_id={"docs": d, "blk": b}, device_id_type=MESH,
        )

    def chunk(ref, index, size, count=None):
        return ref.at[pl.ds(index * size, size if count is None else count)]

    def extra(ref, index, size, skip):
        return ref.at[pl.ds(index * size + skip, size - skip)]

    def ids_copy(q, r, j):
        return copy(ids_send.at[q], ids_recv.at[q], ids_ss.at[q], ids_rs.at[q], docs_at(r), blk_at(j))

    def side_copy(r, j):
        q = r * blocks + j
        into = relay if j else small_recv
        count = ms if j in far else cs
        return copy(
            chunk(small_send, q, cs, count), chunk(into, q, cs, count), side_ss.at[q], side_rs.at[q], docs_at(r), me_b
        )

    def line_copy(r, j):
        q = r * blocks + j
        count = ms if j in far else cs
        return copy(
            chunk(relay, q, cs, count), chunk(small_recv, q, cs, count), small_ss.at[q], small_rs.at[q], me_d, blk_at(j)
        )

    def one_copy(j):
        count = mb if j in far else cb
        return copy(
            chunk(big_send, j, cb, count), chunk(big_all, j, cb, count), one_ss.at[j], one_rs.at[j], me_d, blk_at(j)
        )

    def two_copy(r):
        if r == 1 or r % cores == 0:
            return copy(chunk(big_all, 0, group), chunk(big_all, r, group), two_ss.at[r], two_rs.at[r], docs_at(r), me_b)
        return copy(
            chunk(big_all, r - 1, group), chunk(big_all, r, group), two_ss.at[r], two_rs.at[r], docs_at(1), me_b
        )

    def sover_copy(j, i):
        src = small_over.at[:] if i is None else extra(small_recv, i, cs, ms)
        return copy(
            src, extra(small_recv, j, cs, ms), sover_ss.at[j], sover_rs.at[j], me_d, blk_at(half if i is None else i ^ j)
        )

    def bover_copy(j, i):
        src = big_over.at[:] if i is None else extra(big_all, i, cb, mb)
        return copy(
            src, extra(big_all, j, cb, mb), bover_ss.at[j], bover_rs.at[j], me_d, blk_at(half if i is None else i ^ j)
        )

    def over_copy(r, j):
        q = r * blocks + j
        return copy(
            extra(small_recv, j, cs, ms), extra(small_recv, q, cs, ms), over_ss.at[q], over_rs.at[q], docs_at(r), me_b
        )

    def flag_copy(s):
        return pltpu.make_async_remote_copy(
            src_ref=flags.at[0], dst_ref=flags.at[s], send_sem=flag_ss.at[s], recv_sem=flag_rs.at[s],
            device_id={"slab": lax.rem(me_s + s, slabs)}, device_id_type=MESH,
        )

    hops = []
    held = [half]
    bit = 1
    while bit < half:
        hops += [(j ^ bit, j) for j in held]
        held = held + [j ^ bit for j in held]
        bit *= 2

    def window(index, size):
        return pl.ds(index * size // LANES * LANES, 2 * LANES)

    def sback_copy(q, r, j):
        return copy(
            small_back.at[:, window(q, cs)], back_recv.at[q], sback_ss.at[q], sback_rs.at[q], docs_at(r, -1), blk_at(j)
        )

    def bback_copy(j):
        return copy(
            big_back.at[:, window(j, cb)], back_recv.at[n + j], bback_ss.at[j], bback_rs.at[j], me_d, blk_at(j)
        )

    cluster = cluster_ref[...]
    is_big = cluster < limit
    rest = jnp.maximum(cluster - limit, 0)
    level = rest // n
    owner = lax.rem(rest + 2 * level, n) if tight else lax.rem(rest, n)
    owner_b, owner_d = owner // shards, lax.rem(owner, shards)
    side = lax.rem(owner_d // cores - me_x + chips, chips) * cores + lax.rem(lax.rem(owner_d, cores) - me_c + cores, cores)
    line = owner_b ^ me_b
    big_level = cluster // blocks
    turn = lax.rem(big_level, blocks)
    turn = lax.rem(turn, 2) * half + turn // 2 if tight else 0 * turn
    big_line = lax.rem(lax.rem(cluster, blocks) + turn, blocks) ^ me_b
    bucket = jnp.where(is_big, n + big_line, side * blocks + line)
    local_id = jnp.where(is_big, big_level, level) + 1
    onehot = iota((nb, rows), 0) == bucket
    upper = (iota((rows, rows), 0) < iota((rows, rows), 1)).astype(BF16)
    before = jnp.dot(onehot.astype(BF16), upper, preferred_element_type=F32)
    rank = jnp.sum(jnp.where(onehot, before, 0.0), axis=0, keepdims=True).astype(jnp.int32)
    if tight:
        main = jnp.where(is_big, mb, ms)
        is_far = jnp.where(is_big, big_line, line) >= half
        over = is_far & (rank >= main)
        kinds = jnp.where(over, jnp.where(is_big, 1, 0), -1)
        which = iota((16, rows), 0) == kinds
        before = jnp.dot(which.astype(BF16), upper, preferred_element_type=F32)
        extra_rank = jnp.sum(jnp.where(which, before, 0.0), axis=0, keepdims=True).astype(jnp.int32)
        place = jnp.where(over, main + extra_rank, rank)
        lost = over & (place >= jnp.where(is_big, cb, cs))
        flag = jnp.max(jnp.where(lost, 1.0, 0.0), axis=1, keepdims=True)
    else:
        over = None
        place = rank
    at_place = iota((LANES, rows), 0) == place
    load_rows.wait()
    load_weight.wait()

    def embed(block):
        projected = jnp.dot(block, weight[...], preferred_element_type=F32)
        norm = jnp.sqrt(jnp.sum(projected * projected, axis=1, keepdims=True) + 1e-06)
        return (projected / norm).astype(BF16)

    def choose(slot, base, count):
        return (iota((count, rows), 0) + base == slot).astype(BF16)

    def pick(slot, base, count):
        return jnp.dot(choose(slot, base, count), embedded[...], preferred_element_type=F32).astype(BF16)

    kept = ~over if tight else place >= 0
    big_slot = jnp.where(is_big & kept, big_line * cb + place, -1)
    small_slot = jnp.where(is_big | ~kept, -1, bucket * cs + place)
    wide, few = half * cb, cs - ms
    first = [choose(big_slot, wide, group - wide)]
    if tight:
        first.append(choose(jnp.where(over & is_big, place, -1), mb, cb - mb))
        first.append(choose(jnp.where(over & ~is_big, place, -1), ms, few))
    first = jnp.concatenate(first, axis=0)
    first = embed(jnp.dot(first, pooled[...], preferred_element_type=F32).astype(BF16))
    big_send[wide:group, :] = first[0 : group - wide]
    if tight:
        big_over[...] = first[group - wide : group - wide + cb - mb]
        small_over[...] = first[group - wide + cb - mb :]

    pl.semaphore_wait(barrier, len(straight) + len(others))
    if tight:
        bover_copy(half, None).start()
        sover_copy(half, None).start()
    for j in far:
        one_copy(j).start()
    for j in away:
        pl.semaphore_signal(joined, inc=1, device_id={"blk": blk_at(j)}, device_id_type=MESH)

    embedded[...] = embed(pooled[...])
    order = [r for r in range(cores, shards)] + [r for r in range(1, cores)] + [0]
    span = blocks * cs
    for lo, hi, those in ((half * cs, span, far), (0, half * cs, near)):
        for r in order:
            picked = pick(small_slot, r * span + lo, hi - lo)
            if r:
                small_send[r * span + lo : r * span + hi, :] = picked
            else:
                relay[lo:hi, :] = picked
                if lo == 0:
                    small_recv[0:cs, :] = picked[0:cs]
            for j in those:
                (side_copy if r else line_copy)(r, j).start()
            if r and lo == 0:
                side_copy(r, 0).start()
        if lo:
            big_send[0:wide, :] = pick(big_slot, 0, wide)
            big_all[0:cb, :] = big_send[0:cb, :]
            for j in near:
                one_copy(j).start()

    ids = nt(jnp.where(onehot, local_id.astype(F32), 0.0).astype(BF16), at_place.astype(BF16))
    if tight:
        ids = jnp.where(iota((nb, LANES), 1) == LANES - 1, flag, ids)
    for q in range(n):
        g = n + q % blocks
        ids_send[q] = jnp.concatenate([ids[q : q + 1], ids[g : g + 1]], axis=1)
    ids_recv[0] = ids_send[0]
    for q in range(n + blocks, nb):
        back_recv[q] = jnp.zeros((1, 2 * LANES), F32)
    small_back[...] = jnp.zeros_like(small_back)
    big_back[...] = jnp.zeros_like(big_back)
    start = jnp.where(is_big, lax.rem(big_line * cb, LANES), lax.rem((side * blocks + line) * cs, LANES))
    back_lane = start + place

    if tight:
        for j, i in [(half, None)] + hops:
            bover_copy(j, i).wait_recv()
            for j2, i2 in hops:
                if i2 == j:
                    bover_copy(j2, i2).start()
            sover_copy(j, i).wait_recv()
            for j2, i2 in hops:
                if i2 == j:
                    sover_copy(j2, i2).start()
            for r in order:
                if r:
                    over_copy(r, j).start()

    pl.semaphore_wait(joined, len(away))
    for q, r, j in peers:
        ids_copy(q, r, j).start()
    for r in range(1, shards):
        if r == cores:
            for j in away:
                one_copy(j).wait_recv()
            for r2 in range(1, shards):
                if r2 == 1 or r2 % cores == 0:
                    two_copy(r2).start()
        for j in away:
            side_copy(r, j).wait_recv()
            line_copy(r, j).start()

    for q, r, j in peers:
        ids_copy(q, r, j).wait_recv()
    if tight:
        seen = jnp.max(ids_recv[:, 0, LANES - 1 : LANES], axis=0, keepdims=True)
        flags[0] = jnp.broadcast_to(seen, (1, LANES))
        for s in others:
            flag_copy(s).start()
    total = n * cs
    low = iota((total, n), 1) * cs
    at = iota((total, n), 0)
    inside = (at >= low) & (at < low + cs)
    base = jnp.sum(jnp.where(inside, low, 0).astype(F32), axis=1, keepdims=True).astype(jnp.int32)
    small_lane = iota((total, LANES), 1) == iota((total, LANES), 0) - base
    marks = jnp.dot(inside.astype(BF16), ids_recv[:, 0, 0:LANES].astype(BF16), preferred_element_type=F32)
    marks = jnp.where(small_lane, marks, 0.0)
    small_col = jnp.sum(marks, axis=1, keepdims=True)
    small_row = nt(jnp.ones((8, LANES), BF16), marks.astype(BF16))[0:1]

    big_total = n * cb
    low = iota((big_total, n), 1) * cb
    at = iota((big_total, n), 0)
    inside = (at >= low) & (at < low + cb)
    base = jnp.sum(jnp.where(inside, low, 0).astype(F32), axis=1, keepdims=True).astype(jnp.int32)
    marks = jnp.dot(inside.astype(BF16), ids_recv[:, 0, LANES:].astype(BF16), preferred_element_type=F32)
    big_marks[...] = jnp.where(iota((big_total, LANES), 1) == iota((big_total, LANES), 0) - base, marks, 0.0)

    my_row = nt(jnp.ones((8, LANES), BF16), big_marks[0:group, :].astype(BF16))[0:1]
    best = jnp.full((1, group), -1.0, F32)
    for r in range(shards):
        if r:
            two_copy(r).wait_recv()
            if r % cores == 0 and cores > 1:
                two_copy(r + 1).start()
        theirs = pl.ds(r * group, group)
        scores = nt(big_all[theirs, :], big_all[0:group, :])
        allowed = jnp.sum(big_marks[theirs, :], axis=1, keepdims=True) == my_row
        if r == 0:
            allowed = allowed & (iota((group, group), 0) != iota((group, group), 1))
        best = jnp.maximum(best, jnp.max(jnp.where(allowed, scores, -1.0), axis=0, keepdims=True))
    big_back[:, 0:group] = best
    for j in away:
        bback_copy(j).start()
    back_recv[n] = big_back[:, window(0, cb)]

    def small_best(r0, r1, c0, c1):
        scores = nt(small_recv[r0:r1, :], small_recv[c0:c1, :])
        allowed = small_col[r0:r1] == small_row[:, c0:c1]
        if r0 < c1 and c0 < r1:
            allowed = allowed & (iota((r1 - r0, c1 - c0), 0) + r0 != iota((r1 - r0, c1 - c0), 1) + c0)
        return jnp.max(jnp.where(allowed, scores, -1.0), axis=0, keepdims=True)

    last = [(shards - 1, j) for j in range(blocks)]
    arrivals = [(r, j) for r in range(shards) for j in range(blocks) if (r, j) != (0, 0)]
    if tight:
        for r in range(1, shards):
            for j in far:
                over_copy(r, j).wait_recv()
    for r, j in arrivals:
        if (r, j) not in last:
            (line_copy if j else side_copy)(r, j).wait_recv()
    cut = total - span
    edge = cut // LANES * LANES
    width = next(w for w in (256, 128) if edge % w == 0)
    for c in range(0, edge, width):
        small_back[:, c : c + width] = small_best(0, cut, c, c + width)
    if tight:
        for s in others:
            flag_copy(s).wait_recv()
            flag_copy(s).wait_send()
        flag_ref[...] = jnp.max(flags[:, 0, :], axis=0, keepdims=True)
    else:
        flag_ref[...] = jnp.zeros_like(flag_ref)
    for j in away:
        one_copy(j).wait_send()
    for r in range(1, shards):
        two_copy(r).wait_send()
    for q, r, j in peers:
        ids_copy(q, r, j).wait_send()
        if r:
            side_copy(r, j).wait_send()
        if j and (r, j) not in last:
            line_copy(r, j).wait_send()
    if tight:
        for j, i in [(half, None)] + hops:
            bover_copy(j, i).wait_send()
            sover_copy(j, i).wait_send()
            for r in range(1, shards):
                over_copy(r, j).wait_send()
    for r, j in last:
        (line_copy if j else side_copy)(r, j).wait_recv()
    for c in range(0, edge, width):
        small_back[:, c : c + width] = jnp.maximum(small_back[:, c : c + width], small_best(cut, total, c, c + width))
    small_back[:, edge:total] = small_best(0, total, edge, total)
    for q, r, j in peers:
        sback_copy(q, r, j).start()
    back_recv[0] = small_back[:, window(0, cs)]

    for j in away:
        bback_copy(j).wait_recv()
    for q, r, j in peers:
        sback_copy(q, r, j).wait_recv()
    result = exact_dot(back_recv[:, 0, :], (iota((2 * LANES, rows), 0) == back_lane).astype(F32))
    out_ref[...] = jnp.sum(jnp.where(onehot, result, 0.0), axis=0, keepdims=True)

    for j in away:
        bback_copy(j).wait_send()
    for q, r, j in peers:
        sback_copy(q, r, j).wait_send()
    for r, j in last:
        if j:
            line_copy(r, j).wait_send()


def solution(mesh):
    slabs, shards, blocks = mesh.shape["slab"], mesh.shape["docs"], mesh.shape["blk"]
    n = shards * blocks

    def body(pooled, proj_weight, cluster):
        rows, width = pooled.shape
        feature = proj_weight.shape[1]
        big_count = rows // 4
        cap_big = 2 * big_count // shards
        cap_small = 2 * (rows - big_count) // n
        cs = up(cap_small, 16)
        cb = up(cap_big * (shards // blocks), 16)
        nb = up(n + blocks, 16)
        dma = pltpu.SemaphoreType.DMA

        def call(ms, mb, collective_id):
            return pl.pallas_call(
                functools.partial(kernel, (slabs, shards, blocks, cs, ms, cb, mb)),
                out_shape=(jax.ShapeDtypeStruct((1, rows), F32), jax.ShapeDtypeStruct((1, LANES), F32)),
                in_specs=[
                    pl.BlockSpec(memory_space=pl.ANY),
                    pl.BlockSpec(memory_space=pl.ANY),
                    pl.BlockSpec(memory_space=pltpu.VMEM),
                ],
                out_specs=(pl.BlockSpec(memory_space=pltpu.VMEM), pl.BlockSpec(memory_space=pltpu.VMEM)),
                scratch_shapes=[
                    pltpu.VMEM((rows, width), BF16),
                    pltpu.VMEM((width, feature), BF16),
                    pltpu.VMEM((rows, feature), BF16),
                    pltpu.VMEM((n * cs, feature), BF16),
                    pltpu.VMEM((n * cs, feature), BF16),
                    pltpu.VMEM((n * cs, feature), BF16),
                    pltpu.VMEM((blocks * cb, feature), BF16),
                    pltpu.VMEM((n * cb, feature), BF16),
                    pltpu.VMEM((max(cs - ms, 16), feature), BF16),
                    pltpu.VMEM((max(cb - mb, 16), feature), BF16),
                    pltpu.VMEM((n, 1, 2 * LANES), F32),
                    pltpu.VMEM((n, 1, 2 * LANES), F32),
                    pltpu.VMEM((slabs, 1, LANES), F32),
                    pltpu.VMEM((n * cb, LANES), F32),
                    pltpu.VMEM((1, up(n * cs, LANES) + LANES), F32),
                    pltpu.VMEM((1, up(blocks * cb, LANES) + LANES), F32),
                    pltpu.VMEM((nb, 1, 2 * LANES), F32),
                    dma((2,)), dma((n,)), dma((n,)), dma((n,)), dma((n,)), dma((n,)), dma((n,)),
                    dma((blocks,)), dma((blocks,)), dma((shards,)), dma((shards,)), dma((n,)), dma((n,)),
                    dma((blocks,)), dma((blocks,)), dma((blocks,)), dma((blocks,)), dma((n,)), dma((n,)),
                    dma((blocks,)), dma((blocks,)), dma((slabs,)), dma((slabs,)), pltpu.SemaphoreType.REGULAR,
                ],
                compiler_params=pltpu.CompilerParams(
                    collective_id=collective_id, has_side_effects=True, vmem_limit_bytes=60 * 1024 * 1024
                ),
            )(pooled, proj_weight, cluster.reshape(1, rows))

        ms, mb = up(2 * cs // 3, 16), up(cb // 2, 16)
        if ms < cs and mb < cb:
            best, flag = call(ms, mb, 0)
            best = lax.cond(flag[0, 0] > 0.0, lambda: call(cs, cb, 1)[0], lambda: best)
        else:
            best, _ = call(cs, cb, 0)
        return jnp.maximum(best.reshape(rows), -1.0)

    in_specs = (P(("slab", "docs", "blk"), None), P(), P(("slab", "docs", "blk")))
    out_specs = P(("slab", "docs", "blk"))
    return jax.shard_map(body, mesh=mesh, in_specs=in_specs, out_specs=out_specs, check_vma=False)
```

```python
import functools

import jax
import jax.numpy as jnp
from jax import lax
from jax.experimental import pallas as pl
from jax.experimental.pallas import tpu as pltpu
from jax.sharding import PartitionSpec as P

MESH = pl.DeviceIdType.MESH
BIG_OWN = 4
LANES = 128
F32 = jnp.float32
BF16 = jnp.bfloat16


def up(value, step):
    return -(-value // step) * step


def iota(shape, dim):
    return lax.broadcasted_iota(jnp.int32, shape, dim)


def nt(a, b):
    return lax.dot_general(a, b, (((1,), (1,)), ((), ())), preferred_element_type=F32)


def exact_dot(a, b):
    high = a.astype(BF16)
    rest = a - high.astype(F32)
    middle = rest.astype(BF16)
    low = (rest - middle.astype(F32)).astype(BF16)
    three = jnp.dot(jnp.concatenate([high, middle, low], axis=0), b.astype(BF16), preferred_element_type=F32)
    m = a.shape[0]
    return three[:m] + three[m : 2 * m] + three[2 * m :]


def kernel(
    dims, pooled_hbm, weight_hbm, cluster_ref, out_ref, flag_ref,
    pooled, weight, embedded, small_send, relay, small_recv, big_send, big_all, big_over,
    ids_send, ids_recv, flags, big_marks, small_back, big_back, back_recv, at_lane,
    in_sem, ids_ss, ids_rs, side_ss, side_rs, small_ss, small_rs, one_ss, one_rs, two_ss, two_rs,
    sback_ss, sback_rs, bback_ss, bback_rs, over_ss, over_rs, bover_ss, bover_rs, flag_ss, flag_rs, joined,
):
    slabs, shards, blocks, cs, ms, cb, mb = dims
    tight = ms < cs
    n = shards * blocks
    rows = pooled.shape[0]
    nb = back_recv.shape[0]
    limit = BIG_OWN * shards
    cores = 2 if shards % 2 == 0 else 1
    chips = shards // cores
    half = blocks // 2
    me_s, me_d, me_b = lax.axis_index("slab"), lax.axis_index("docs"), lax.axis_index("blk")
    me_x, me_c = me_d // cores, lax.rem(me_d, cores)
    group = blocks * cb
    far = [j for j in range(blocks) if j & half]
    near = [j for j in range(1, blocks) if not j & half]
    away = far + near

    def docs_at(r, sign=1):
        dx, dc = r // cores, r % cores
        return lax.rem(me_x + sign * dx + chips, chips) * cores + lax.rem(me_c + dc, cores)

    def blk_at(j):
        return me_b ^ j

    peers = [(r * blocks + j, r, j) for j in away + [0] for r in range(shards - 1, -1, -1) if (r, j) != (0, 0)]

    load_rows = pltpu.make_async_copy(pooled_hbm, pooled, in_sem.at[0])
    load_weight = pltpu.make_async_copy(weight_hbm, weight, in_sem.at[1])
    load_rows.start()
    load_weight.start()
    barrier = pltpu.get_barrier_semaphore()
    straight = [(r, j) for _, r, j in peers if r == 0 or j == 0]
    for r, j in straight:
        pl.semaphore_signal(
            barrier, inc=1, device_id={"docs": docs_at(r), "blk": blk_at(j)}, device_id_type=MESH
        )
    others = range(1, slabs) if tight else ()
    for s in others:
        pl.semaphore_signal(barrier, inc=1, device_id={"slab": lax.rem(me_s + s, slabs)}, device_id_type=MESH)

    def copy(src, dst, ssem, rsem, d, b):
        return pltpu.make_async_remote_copy(
            src_ref=src, dst_ref=dst, send_sem=ssem, recv_sem=rsem,
            device_id={"docs": d, "blk": b}, device_id_type=MESH,
        )

    def chunk(ref, index, size, count=None):
        return ref.at[pl.ds(index * size, size if count is None else count)]

    def extra(ref, index, size, skip):
        return ref.at[pl.ds(index * size + skip, size - skip)]

    def ids_copy(q, r, j):
        return copy(ids_send.at[q], ids_recv.at[q], ids_ss.at[q], ids_rs.at[q], docs_at(r), blk_at(j))

    def side_copy(r, j):
        q = r * blocks + j
        into = relay if j else small_recv
        count = ms if j in far else cs
        return copy(
            chunk(small_send, q, cs, count), chunk(into, q, cs, count), side_ss.at[q], side_rs.at[q], docs_at(r), me_b
        )

    def line_copy(r, j):
        q = r * blocks + j
        count = ms if j in far else cs
        return copy(
            chunk(relay, q, cs, count), chunk(small_recv, q, cs, count), small_ss.at[q], small_rs.at[q], me_d, blk_at(j)
        )

    def one_copy(j):
        count = mb if j in far else cb
        return copy(
            chunk(big_send, j, cb, count), chunk(big_all, j, cb, count), one_ss.at[j], one_rs.at[j], me_d, blk_at(j)
        )

    def two_copy(r):
        if r == 1 or r % cores == 0:
            return copy(chunk(big_all, 0, group), chunk(big_all, r, group), two_ss.at[r], two_rs.at[r], docs_at(r), me_b)
        return copy(
            chunk(big_all, r - 1, group), chunk(big_all, r, group), two_ss.at[r], two_rs.at[r], docs_at(1), me_b
        )

    def bover_copy(j, i):
        src = big_over.at[:] if i is None else extra(big_all, i, cb, mb)
        return copy(
            src, extra(big_all, j, cb, mb), bover_ss.at[j], bover_rs.at[j], me_d, blk_at(half if i is None else i ^ j)
        )

    def over_copy(r, j):
        q = r * blocks + j
        direct = r == 1 or r % cores == 0
        i = j if direct else q - blocks
        return copy(
            extra(small_recv, i, cs, ms), extra(small_recv, q, cs, ms), over_ss.at[q], over_rs.at[q],
            docs_at(r if direct else 1), me_b,
        )

    def flag_copy(s):
        return pltpu.make_async_remote_copy(
            src_ref=flags.at[0], dst_ref=flags.at[s], send_sem=flag_ss.at[s], recv_sem=flag_rs.at[s],
            device_id={"slab": lax.rem(me_s + s, slabs)}, device_id_type=MESH,
        )

    hops = []
    held = [half]
    bit = 1
    while bit < half:
        hops += [(j ^ bit, j) for j in held]
        held = held + [j ^ bit for j in held]
        bit *= 2

    def window(index, size):
        return pl.ds(index * size // LANES * LANES, 2 * LANES)

    def sback_copy(q, r, j):
        return copy(
            small_back.at[:, window(q, cs)], back_recv.at[q], sback_ss.at[q], sback_rs.at[q], docs_at(r, -1), blk_at(j)
        )

    def bback_copy(j):
        return copy(
            big_back.at[:, window(j, cb)], back_recv.at[n + j], bback_ss.at[j], bback_rs.at[j], me_d, blk_at(j)
        )

    cluster = cluster_ref[...]
    is_big = cluster < limit
    rest = jnp.maximum(cluster - limit, 0)
    level = rest // n
    owner = lax.rem(rest + 2 * level, n) if tight else lax.rem(rest, n)
    owner_b, owner_d = owner // shards, lax.rem(owner, shards)
    side = lax.rem(owner_d // cores - me_x + chips, chips) * cores + lax.rem(lax.rem(owner_d, cores) - me_c + cores, cores)
    line = owner_b ^ me_b
    big_level = cluster // blocks
    turn = lax.rem(big_level, blocks)
    turn = lax.rem(turn, 2) * half + turn // 2 if tight else 0 * turn
    big_line = lax.rem(lax.rem(cluster, blocks) + turn, blocks) ^ me_b
    bucket = jnp.where(is_big, n + big_line, side * blocks + line)
    local_id = jnp.where(is_big, big_level, level) + 1
    onehot = iota((nb, rows), 0) == bucket
    upper = (iota((rows, rows), 0) < iota((rows, rows), 1)).astype(BF16)
    before = jnp.dot(onehot.astype(BF16), upper, preferred_element_type=F32)
    rank = jnp.sum(jnp.where(onehot, before, 0.0), axis=0, keepdims=True).astype(jnp.int32)
    if tight:
        main = jnp.where(is_big, mb, ms)
        is_far = jnp.where(is_big, big_line, line) >= half
        over = is_far & (rank >= main)
        kinds = jnp.where(over, jnp.where(is_big, 1, 0), -1)
        which = iota((16, rows), 0) == kinds
        before = jnp.dot(which.astype(BF16), upper, preferred_element_type=F32)
        extra_rank = jnp.sum(jnp.where(which, before, 0.0), axis=0, keepdims=True).astype(jnp.int32)
        spare = cb - mb
        count = jnp.sum(jnp.where(over, 1.0, 0.0), axis=1, keepdims=True)
        spot = jnp.where(is_big, spare - 1 - extra_rank, extra_rank)
        place = jnp.where(over, main + spot, rank)
        lost = over & ((count > spare) | (extra_rank >= jnp.where(is_big, spare, cs - ms)))
        flag = jnp.max(jnp.where(lost, 1.0, 0.0), axis=1, keepdims=True)
    else:
        over = None
        place = rank
    at_place = iota((LANES, rows), 0) == place
    load_rows.wait()
    load_weight.wait()

    def embed(block):
        projected = jnp.dot(block, weight[...], preferred_element_type=F32)
        norm = jnp.sqrt(jnp.sum(projected * projected, axis=1, keepdims=True) + 1e-06)
        return (projected / norm).astype(BF16)

    def choose(slot, base, count):
        return (iota((count, rows), 0) + base == slot).astype(BF16)

    def pick(slot, base, count):
        return jnp.dot(choose(slot, base, count), embedded[...], preferred_element_type=F32).astype(BF16)

    kept = ~over if tight else place >= 0
    big_slot = jnp.where(is_big & kept, big_line * cb + place, -1)
    small_slot = jnp.where(is_big | ~kept, -1, bucket * cs + place)
    wide, few = half * cb, cs - ms
    first = [choose(big_slot, wide, group - wide)]
    if tight:
        first.append(choose(jnp.where(over, spot, -1), 0, cb - mb))
    first = jnp.concatenate(first, axis=0)
    first = embed(jnp.dot(first, pooled[...], preferred_element_type=F32).astype(BF16))
    big_send[wide:group, :] = first[0 : group - wide]
    if tight:
        big_over[...] = first[group - wide :]

    pl.semaphore_wait(barrier, len(straight) + len(others))
    if tight:
        bover_copy(half, None).start()
    for j in far:
        one_copy(j).start()
    for j in away:
        pl.semaphore_signal(joined, inc=1, device_id={"blk": blk_at(j)}, device_id_type=MESH)

    embedded[...] = embed(pooled[...])
    order = [r for r in range(cores, shards)] + [r for r in range(1, cores)] + [0]
    span = blocks * cs
    for lo, hi, those in ((half * cs, span, far), (0, half * cs, near)):
        for r in order:
            picked = pick(small_slot, r * span + lo, hi - lo)
            if r:
                small_send[r * span + lo : r * span + hi, :] = picked
            else:
                relay[lo:hi, :] = picked
                if lo == 0:
                    small_recv[0:cs, :] = picked[0:cs]
            for j in those:
                (side_copy if r else line_copy)(r, j).start()
            if r and lo == 0:
                side_copy(r, 0).start()
        if lo:
            ids = nt(jnp.where(onehot, local_id.astype(F32), 0.0).astype(BF16), at_place.astype(BF16))
            if tight:
                ids = jnp.where(iota((nb, LANES), 1) == LANES - 1, flag, ids)
            for q in range(n):
                g = n + q % blocks
                ids_send[q] = jnp.concatenate([ids[q : q + 1], ids[g : g + 1]], axis=1)
            ids_recv[0] = ids_send[0]
            for q in range(n + blocks, nb):
                back_recv[q] = jnp.zeros((1, 2 * LANES), F32)
            small_back[...] = jnp.zeros_like(small_back)
            big_back[...] = jnp.zeros_like(big_back)
            start = jnp.where(is_big, lax.rem(big_line * cb, LANES), lax.rem((side * blocks + line) * cs, LANES))
            at_lane[...] = (iota((2 * LANES, rows), 0) == start + place).astype(BF16)

            pl.semaphore_wait(joined, len(away))
            for q, r, j in peers:
                ids_copy(q, r, j).start()
            big_send[0:wide, :] = pick(big_slot, 0, wide)
            big_all[0:cb, :] = big_send[0:cb, :]
            for j in near:
                one_copy(j).start()

    if tight:
        for j, i in [(half, None)] + hops:
            bover_copy(j, i).wait_recv()
            for j2, i2 in hops:
                if i2 == j:
                    bover_copy(j2, i2).start()
            small_recv[j * cs + ms : (j + 1) * cs, :] = big_all[j * cb + mb : j * cb + mb + few, :]
            for r in order:
                if r == 1 or r % cores == 0 and r:
                    over_copy(r, j).start()

    for j in away:
        one_copy(j).wait_recv()
    for r in range(1, shards):
        if r == 1 or r % cores == 0:
            two_copy(r).start()
    for r in range(1, shards):
        for j in far:
            side_copy(r, j).wait_recv()
            line_copy(r, j).start()
    for r in range(1, shards):
        for j in near:
            side_copy(r, j).wait_recv()
            line_copy(r, j).start()
    if tight:
        for r in range(cores, shards):
            if r % cores:
                for j in far:
                    over_copy(r - 1, j).wait_recv()
                    over_copy(r, j).start()
    for q, r, j in peers:
        ids_copy(q, r, j).wait_recv()
    if tight:
        seen = jnp.max(ids_recv[:, 0, LANES - 1 : LANES], axis=0, keepdims=True)
        flags[0] = jnp.broadcast_to(seen, (1, LANES))
        for s in others:
            flag_copy(s).start()
    total = n * cs
    low = iota((total, n), 1) * cs
    at = iota((total, n), 0)
    inside = (at >= low) & (at < low + cs)
    base = jnp.sum(jnp.where(inside, low, 0).astype(F32), axis=1, keepdims=True).astype(jnp.int32)
    small_lane = iota((total, LANES), 1) == iota((total, LANES), 0) - base
    marks = jnp.dot(inside.astype(BF16), ids_recv[:, 0, 0:LANES].astype(BF16), preferred_element_type=F32)
    marks = jnp.where(small_lane, marks, 0.0)
    small_col = jnp.sum(marks, axis=1, keepdims=True)
    small_row = nt(jnp.ones((8, LANES), BF16), marks.astype(BF16))[0:1]

    big_total = n * cb
    low = iota((big_total, n), 1) * cb
    at = iota((big_total, n), 0)
    inside = (at >= low) & (at < low + cb)
    base = jnp.sum(jnp.where(inside, low, 0).astype(F32), axis=1, keepdims=True).astype(jnp.int32)
    marks = jnp.dot(inside.astype(BF16), ids_recv[:, 0, LANES:].astype(BF16), preferred_element_type=F32)
    big_marks[...] = jnp.where(iota((big_total, LANES), 1) == iota((big_total, LANES), 0) - base, marks, 0.0)

    my_row = nt(jnp.ones((8, LANES), BF16), big_marks[0:group, :].astype(BF16))[0:1]
    best = jnp.full((1, group), -1.0, F32)
    for r in range(shards):
        if r:
            two_copy(r).wait_recv()
            if r % cores == 0 and cores > 1:
                two_copy(r + 1).start()
        theirs = pl.ds(r * group, group)
        scores = nt(big_all[theirs, :], big_all[0:group, :])
        allowed = jnp.sum(big_marks[theirs, :], axis=1, keepdims=True) == my_row
        if r == 0:
            allowed = allowed & (iota((group, group), 0) != iota((group, group), 1))
        best = jnp.maximum(best, jnp.max(jnp.where(allowed, scores, -1.0), axis=0, keepdims=True))
    big_back[:, 0:group] = best
    for j in away:
        bback_copy(j).start()
    back_recv[n] = big_back[:, window(0, cb)]

    def small_best(r0, r1, c0, c1):
        scores = nt(small_recv[r0:r1, :], small_recv[c0:c1, :])
        allowed = small_col[r0:r1] == small_row[:, c0:c1]
        if r0 < c1 and c0 < r1:
            allowed = allowed & (iota((r1 - r0, c1 - c0), 0) + r0 != iota((r1 - r0, c1 - c0), 1) + c0)
        return jnp.max(jnp.where(allowed, scores, -1.0), axis=0, keepdims=True)

    last = [(shards - 1, j) for j in range(blocks)]
    arrivals = [(r, j) for r in range(shards) for j in range(blocks) if (r, j) != (0, 0)]
    if tight:
        for r in range(1, shards):
            for j in far:
                if r % cores or r + 1 == shards or cores == 1:
                    over_copy(r, j).wait_recv()
    for r, j in arrivals:
        if (r, j) not in last:
            (line_copy if j else side_copy)(r, j).wait_recv()
    cut = total - span
    edge = cut // LANES * LANES
    width = next(w for w in (256, 128) if edge % w == 0)
    for c in range(0, edge, width):
        small_back[:, c : c + width] = small_best(0, cut, c, c + width)
    if tight:
        for s in others:
            flag_copy(s).wait_recv()
            flag_copy(s).wait_send()
        flag_ref[...] = jnp.max(flags[:, 0, :], axis=0, keepdims=True)
    else:
        flag_ref[...] = jnp.zeros_like(flag_ref)
    for j in away:
        one_copy(j).wait_send()
    for r in range(1, shards):
        two_copy(r).wait_send()
    for q, r, j in peers:
        ids_copy(q, r, j).wait_send()
        if r:
            side_copy(r, j).wait_send()
        if j and (r, j) not in last:
            line_copy(r, j).wait_send()
    if tight:
        for j, i in [(half, None)] + hops:
            bover_copy(j, i).wait_send()
            for r in range(1, shards):
                over_copy(r, j).wait_send()
    for r, j in last:
        (line_copy if j else side_copy)(r, j).wait_recv()
    for c in range(0, edge, width):
        small_back[:, c : c + width] = jnp.maximum(small_back[:, c : c + width], small_best(cut, total, c, c + width))
    small_back[:, edge:total] = small_best(0, total, edge, total)
    for q, r, j in peers:
        sback_copy(q, r, j).start()
    back_recv[0] = small_back[:, window(0, cs)]

    for j in away:
        bback_copy(j).wait_recv()
    for q, r, j in peers:
        sback_copy(q, r, j).wait_recv()
    result = exact_dot(back_recv[:, 0, :], at_lane[...])
    out_ref[...] = jnp.sum(jnp.where(onehot, result, 0.0), axis=0, keepdims=True)

    for j in away:
        bback_copy(j).wait_send()
    for q, r, j in peers:
        sback_copy(q, r, j).wait_send()
    for r, j in last:
        if j:
            line_copy(r, j).wait_send()


def solution(mesh):
    slabs, shards, blocks = mesh.shape["slab"], mesh.shape["docs"], mesh.shape["blk"]
    n = shards * blocks

    def body(pooled, proj_weight, cluster):
        rows, width = pooled.shape
        feature = proj_weight.shape[1]
        big_count = rows // 4
        cap_big = 2 * big_count // shards
        cap_small = 2 * (rows - big_count) // n
        cs = up(cap_small, 16)
        cb = up(cap_big * (shards // blocks), 16)
        nb = up(n + blocks, 16)
        dma = pltpu.SemaphoreType.DMA

        def call(ms, mb, collective_id):
            return pl.pallas_call(
                functools.partial(kernel, (slabs, shards, blocks, cs, ms, cb, mb)),
                out_shape=(jax.ShapeDtypeStruct((1, rows), F32), jax.ShapeDtypeStruct((1, LANES), F32)),
                in_specs=[
                    pl.BlockSpec(memory_space=pl.ANY),
                    pl.BlockSpec(memory_space=pl.ANY),
                    pl.BlockSpec(memory_space=pltpu.VMEM),
                ],
                out_specs=(pl.BlockSpec(memory_space=pltpu.VMEM), pl.BlockSpec(memory_space=pltpu.VMEM)),
                scratch_shapes=[
                    pltpu.VMEM((rows, width), BF16),
                    pltpu.VMEM((width, feature), BF16),
                    pltpu.VMEM((rows, feature), BF16),
                    pltpu.VMEM((n * cs, feature), BF16),
                    pltpu.VMEM((n * cs, feature), BF16),
                    pltpu.VMEM((n * cs, feature), BF16),
                    pltpu.VMEM((blocks * cb, feature), BF16),
                    pltpu.VMEM((n * cb, feature), BF16),
                    pltpu.VMEM((max(cb - mb, 16), feature), BF16),
                    pltpu.VMEM((n, 1, 2 * LANES), F32),
                    pltpu.VMEM((n, 1, 2 * LANES), F32),
                    pltpu.VMEM((slabs, 1, LANES), F32),
                    pltpu.VMEM((n * cb, LANES), F32),
                    pltpu.VMEM((1, up(n * cs, LANES) + LANES), F32),
                    pltpu.VMEM((1, up(blocks * cb, LANES) + LANES), F32),
                    pltpu.VMEM((nb, 1, 2 * LANES), F32),
                    pltpu.VMEM((2 * LANES, rows), BF16),
                    dma((2,)), dma((n,)), dma((n,)), dma((n,)), dma((n,)), dma((n,)), dma((n,)),
                    dma((blocks,)), dma((blocks,)), dma((shards,)), dma((shards,)), dma((n,)), dma((n,)),
                    dma((blocks,)), dma((blocks,)), dma((n,)), dma((n,)),
                    dma((blocks,)), dma((blocks,)), dma((slabs,)), dma((slabs,)), pltpu.SemaphoreType.REGULAR,
                ],
                compiler_params=pltpu.CompilerParams(
                    collective_id=collective_id, has_side_effects=True, vmem_limit_bytes=60 * 1024 * 1024
                ),
            )(pooled, proj_weight, cluster.reshape(1, rows))

        ms, mb = up(2 * cs // 3, 16), up(cb // 2, 16)
        if ms < cs and mb < cb and cs - ms <= cb - mb:
            best, flag = call(ms, mb, 0)
            best = lax.cond(flag[0, 0] > 0.0, lambda: call(cs, cb, 1)[0], lambda: best)
        else:
            best, _ = call(cs, cb, 0)
        return jnp.maximum(best.reshape(rows), -1.0)

    in_specs = (P(("slab", "docs", "blk"), None), P(), P(("slab", "docs", "blk")))
    out_specs = P(("slab", "docs", "blk"))
    return jax.shard_map(body, mesh=mesh, in_specs=in_specs, out_specs=out_specs, check_vma=False)
```

```python
import functools

import jax
import jax.numpy as jnp
from jax import lax
from jax.experimental import pallas as pl
from jax.experimental.pallas import tpu as pltpu
from jax.sharding import PartitionSpec as P

MESH = pl.DeviceIdType.MESH
BIG_OWN = 4
LANES = 128
F32 = jnp.float32
BF16 = jnp.bfloat16


def up(value, step):
    return -(-value // step) * step


def iota(shape, dim):
    return lax.broadcasted_iota(jnp.int32, shape, dim)


def nt(a, b):
    return lax.dot_general(a, b, (((1,), (1,)), ((), ())), preferred_element_type=F32)


def exact_dot(a, b):
    high = a.astype(BF16)
    rest = a - high.astype(F32)
    middle = rest.astype(BF16)
    low = (rest - middle.astype(F32)).astype(BF16)
    three = jnp.dot(jnp.concatenate([high, middle, low], axis=0), b.astype(BF16), preferred_element_type=F32)
    m = a.shape[0]
    return three[:m] + three[m : 2 * m] + three[2 * m :]


def kernel(
    dims, pooled_hbm, weight_hbm, cluster_ref, out_ref, flag_ref,
    pooled, weight, embedded, small_send, relay, small_recv, big_send, big_all, big_over,
    ids_send, ids_recv, flags, big_marks, small_back, big_back, back_recv, at_lane,
    in_sem, ids_ss, ids_rs, side_ss, side_rs, small_ss, small_rs, one_ss, one_rs, two_ss, two_rs,
    sback_ss, sback_rs, bback_ss, bback_rs, over_ss, over_rs, bover_ss, bover_rs, flag_ss, flag_rs, joined,
):
    slabs, shards, blocks, cs, ms, cb, mb = dims
    tight = ms < cs
    n = shards * blocks
    rows = pooled.shape[0]
    nb = back_recv.shape[0]
    limit = BIG_OWN * shards
    cores = 2 if shards % 2 == 0 else 1
    chips = shards // cores
    half = blocks // 2
    me_s, me_d, me_b = lax.axis_index("slab"), lax.axis_index("docs"), lax.axis_index("blk")
    me_x, me_c = me_d // cores, lax.rem(me_d, cores)
    group = blocks * cb
    far = [j for j in range(blocks) if j & half]
    near = [j for j in range(1, blocks) if not j & half]
    away = far + near

    def docs_at(r, sign=1):
        dx, dc = r // cores, r % cores
        return lax.rem(me_x + sign * dx + chips, chips) * cores + lax.rem(me_c + dc, cores)

    def blk_at(j):
        return me_b ^ j

    peers = [(r * blocks + j, r, j) for j in away + [0] for r in range(shards - 1, -1, -1) if (r, j) != (0, 0)]

    load_rows = pltpu.make_async_copy(pooled_hbm, pooled, in_sem.at[0])
    load_weight = pltpu.make_async_copy(weight_hbm, weight, in_sem.at[1])
    load_rows.start()
    load_weight.start()
    barrier = pltpu.get_barrier_semaphore()
    straight = [(r, j) for _, r, j in peers if r == 0 or j == 0]
    for r, j in straight:
        pl.semaphore_signal(
            barrier, inc=1, device_id={"docs": docs_at(r), "blk": blk_at(j)}, device_id_type=MESH
        )
    others = range(1, slabs) if tight else ()
    for s in others:
        pl.semaphore_signal(barrier, inc=1, device_id={"slab": lax.rem(me_s + s, slabs)}, device_id_type=MESH)

    def copy(src, dst, ssem, rsem, d, b):
        return pltpu.make_async_remote_copy(
            src_ref=src, dst_ref=dst, send_sem=ssem, recv_sem=rsem,
            device_id={"docs": d, "blk": b}, device_id_type=MESH,
        )

    def chunk(ref, index, size, count=None):
        return ref.at[pl.ds(index * size, size if count is None else count)]

    def extra(ref, index, size, skip):
        return ref.at[pl.ds(index * size + skip, size - skip)]

    def ids_copy(q, r, j):
        return copy(ids_send.at[q], ids_recv.at[q], ids_ss.at[q], ids_rs.at[q], docs_at(r), blk_at(j))

    def side_copy(r, j):
        q = r * blocks + j
        into = relay if j else small_recv
        count = ms if j in far else cs
        return copy(
            chunk(small_send, q, cs, count), chunk(into, q, cs, count), side_ss.at[q], side_rs.at[q], docs_at(r), me_b
        )

    def line_copy(r, j):
        q = r * blocks + j
        count = ms if j in far else cs
        return copy(
            chunk(relay, q, cs, count), chunk(small_recv, q, cs, count), small_ss.at[q], small_rs.at[q], me_d, blk_at(j)
        )

    def one_copy(j):
        count = mb if j in far else cb
        return copy(
            chunk(big_send, j, cb, count), chunk(big_all, j, cb, count), one_ss.at[j], one_rs.at[j], me_d, blk_at(j)
        )

    def two_copy(r):
        if r == 1 or r % cores == 0:
            return copy(chunk(big_all, 0, group), chunk(big_all, r, group), two_ss.at[r], two_rs.at[r], docs_at(r), me_b)
        return copy(
            chunk(big_all, r - 1, group), chunk(big_all, r, group), two_ss.at[r], two_rs.at[r], docs_at(1), me_b
        )

    def bover_copy(j, i):
        src = big_over.at[:] if i is None else extra(big_all, i, cb, mb)
        return copy(
            src, extra(big_all, j, cb, mb), bover_ss.at[j], bover_rs.at[j], me_d, blk_at(half if i is None else i ^ j)
        )

    def over_copy(r, j):
        q = r * blocks + j
        direct = r == 1 or r % cores == 0
        i = j if direct else q - blocks
        return copy(
            extra(small_recv, i, cs, ms), extra(small_recv, q, cs, ms), over_ss.at[q], over_rs.at[q],
            docs_at(r if direct else 1), me_b,
        )

    def flag_copy(s):
        return pltpu.make_async_remote_copy(
            src_ref=flags.at[0], dst_ref=flags.at[s], send_sem=flag_ss.at[s], recv_sem=flag_rs.at[s],
            device_id={"slab": lax.rem(me_s + s, slabs)}, device_id_type=MESH,
        )

    hops = []
    held = [half]
    bit = 1
    while bit < half:
        hops += [(j ^ bit, j) for j in held]
        held = held + [j ^ bit for j in held]
        bit *= 2

    def window(index, size):
        return pl.ds(index * size // LANES * LANES, 2 * LANES)

    def sback_copy(q, r, j):
        return copy(
            small_back.at[:, window(q, cs)], back_recv.at[q], sback_ss.at[q], sback_rs.at[q], docs_at(r, -1), blk_at(j)
        )

    def bback_copy(j):
        return copy(
            big_back.at[:, window(j, cb)], back_recv.at[n + j], bback_ss.at[j], bback_rs.at[j], me_d, blk_at(j)
        )

    cluster = cluster_ref[...]
    is_big = cluster < limit
    rest = jnp.maximum(cluster - limit, 0)
    level = rest // n
    owner = lax.rem(rest + 2 * level, n) if tight else lax.rem(rest, n)
    owner_b, owner_d = owner // shards, lax.rem(owner, shards)
    side = lax.rem(owner_d // cores - me_x + chips, chips) * cores + lax.rem(lax.rem(owner_d, cores) - me_c + cores, cores)
    line = owner_b ^ me_b
    big_level = cluster // blocks
    turn = lax.rem(big_level, blocks)
    turn = lax.rem(turn, 2) * half + turn // 2 if tight else 0 * turn
    big_line = lax.rem(lax.rem(cluster, blocks) + turn, blocks) ^ me_b
    bucket = jnp.where(is_big, n + big_line, side * blocks + line)
    local_id = jnp.where(is_big, big_level, level) + 1
    onehot = iota((nb, rows), 0) == bucket
    upper = (iota((rows, rows), 0) < iota((rows, rows), 1)).astype(BF16)
    before = jnp.dot(onehot.astype(BF16), upper, preferred_element_type=F32)
    rank = jnp.sum(jnp.where(onehot, before, 0.0), axis=0, keepdims=True).astype(jnp.int32)
    if tight:
        main = jnp.where(is_big, mb, ms)
        is_far = jnp.where(is_big, big_line, line) >= half
        over = is_far & (rank >= main)
        kinds = jnp.where(over, jnp.where(is_big, 1, 0), -1)
        which = iota((16, rows), 0) == kinds
        before = jnp.dot(which.astype(BF16), upper, preferred_element_type=F32)
        extra_rank = jnp.sum(jnp.where(which, before, 0.0), axis=0, keepdims=True).astype(jnp.int32)
        spare = cb - mb
        count = jnp.sum(jnp.where(over, 1.0, 0.0), axis=1, keepdims=True)
        spot = jnp.where(is_big, spare - 1 - extra_rank, extra_rank)
        place = jnp.where(over, main + spot, rank)
        lost = over & ((count > spare) | (extra_rank >= jnp.where(is_big, spare, cs - ms)))
        flag = jnp.max(jnp.where(lost, 1.0, 0.0), axis=1, keepdims=True)
    else:
        over = None
        place = rank
    at_place = iota((LANES, rows), 0) == place
    load_rows.wait()
    load_weight.wait()

    def embed(block):
        projected = jnp.dot(block, weight[...], preferred_element_type=F32)
        norm = jnp.sqrt(jnp.sum(projected * projected, axis=1, keepdims=True) + 1e-06)
        return (projected / norm).astype(BF16)

    def choose(slot, base, count):
        return (iota((count, rows), 0) + base == slot).astype(BF16)

    def pick(slot, base, count):
        return jnp.dot(choose(slot, base, count), embedded[...], preferred_element_type=F32).astype(BF16)

    kept = ~over if tight else place >= 0
    big_slot = jnp.where(is_big & kept, big_line * cb + place, -1)
    small_slot = jnp.where(is_big | ~kept, -1, bucket * cs + place)
    wide, few = half * cb, cs - ms
    first = [choose(big_slot, wide, group - wide)]
    if tight:
        first.append(choose(jnp.where(over, spot, -1), 0, cb - mb))
    first = jnp.concatenate(first, axis=0)
    first = embed(jnp.dot(first, pooled[...], preferred_element_type=F32).astype(BF16))
    big_send[wide:group, :] = first[0 : group - wide]
    if tight:
        big_over[...] = first[group - wide :]

    pl.semaphore_wait(barrier, len(straight) + len(others))
    if tight:
        bover_copy(half, None).start()
    for j in far:
        one_copy(j).start()
    for j in away:
        pl.semaphore_signal(joined, inc=1, device_id={"blk": blk_at(j)}, device_id_type=MESH)

    embedded[...] = embed(pooled[...])
    order = [r for r in range(cores, shards)] + [r for r in range(1, cores)] + [0]
    span = blocks * cs
    for lo, hi, those in ((half * cs, span, far), (0, half * cs, near)):
        for r in order:
            picked = pick(small_slot, r * span + lo, hi - lo)
            if r:
                small_send[r * span + lo : r * span + hi, :] = picked
            else:
                relay[lo:hi, :] = picked
                if lo == 0:
                    small_recv[0:cs, :] = picked[0:cs]
            for j in those:
                (side_copy if r else line_copy)(r, j).start()
            if r and lo == 0:
                side_copy(r, 0).start()
        if lo:
            ids = nt(jnp.where(onehot, local_id.astype(F32), 0.0).astype(BF16), at_place.astype(BF16))
            if tight:
                ids = jnp.where(iota((nb, LANES), 1) == LANES - 1, flag, ids)
            for q in range(n):
                g = n + q % blocks
                ids_send[q] = jnp.concatenate([ids[q : q + 1], ids[g : g + 1]], axis=1)
            ids_recv[0] = ids_send[0]
            for q in range(n + blocks, nb):
                back_recv[q] = jnp.zeros((1, 2 * LANES), F32)
            small_back[...] = jnp.zeros_like(small_back)
            big_back[...] = jnp.zeros_like(big_back)
            start = jnp.where(is_big, lax.rem(big_line * cb, LANES), lax.rem((side * blocks + line) * cs, LANES))
            at_lane[...] = (iota((2 * LANES, rows), 0) == start + place).astype(BF16)

            pl.semaphore_wait(joined, len(away))
            for q, r, j in peers:
                ids_copy(q, r, j).start()
            big_send[0:wide, :] = pick(big_slot, 0, wide)
            big_all[0:cb, :] = big_send[0:cb, :]
            for j in near:
                one_copy(j).start()

    if tight:
        for j, i in [(half, None)] + hops:
            bover_copy(j, i).wait_recv()
            for j2, i2 in hops:
                if i2 == j:
                    bover_copy(j2, i2).start()
            small_recv[j * cs + ms : (j + 1) * cs, :] = big_all[j * cb + mb : j * cb + mb + few, :]
            for r in order:
                if r == 1 or r % cores == 0 and r:
                    over_copy(r, j).start()

    for j in away:
        one_copy(j).wait_recv()
    for r in range(1, shards):
        if r == 1 or r % cores == 0:
            two_copy(r).start()
    for r in range(1, shards):
        for j in far:
            side_copy(r, j).wait_recv()
            line_copy(r, j).start()
    for r in range(1, shards):
        for j in near:
            side_copy(r, j).wait_recv()
            line_copy(r, j).start()
    if tight:
        for r in range(cores, shards):
            if r % cores:
                for j in far:
                    over_copy(r - 1, j).wait_recv()
                    over_copy(r, j).start()
    for q, r, j in peers:
        ids_copy(q, r, j).wait_recv()
    if tight:
        seen = jnp.max(ids_recv[:, 0, LANES - 1 : LANES], axis=0, keepdims=True)
        flags[0] = jnp.broadcast_to(seen, (1, LANES))
        for s in others:
            flag_copy(s).start()
    total = n * cs
    low = iota((total, n), 1) * cs
    at = iota((total, n), 0)
    inside = (at >= low) & (at < low + cs)
    base = jnp.sum(jnp.where(inside, low, 0).astype(F32), axis=1, keepdims=True).astype(jnp.int32)
    small_lane = iota((total, LANES), 1) == iota((total, LANES), 0) - base
    marks = jnp.dot(inside.astype(BF16), ids_recv[:, 0, 0:LANES].astype(BF16), preferred_element_type=F32)
    marks = jnp.where(small_lane, marks, 0.0)
    small_col = jnp.sum(marks, axis=1, keepdims=True)
    small_row = nt(jnp.ones((8, LANES), BF16), marks.astype(BF16))[0:1]

    big_total = n * cb
    low = iota((big_total, n), 1) * cb
    at = iota((big_total, n), 0)
    inside = (at >= low) & (at < low + cb)
    base = jnp.sum(jnp.where(inside, low, 0).astype(F32), axis=1, keepdims=True).astype(jnp.int32)
    marks = jnp.dot(inside.astype(BF16), ids_recv[:, 0, LANES:].astype(BF16), preferred_element_type=F32)
    big_marks[...] = jnp.where(iota((big_total, LANES), 1) == iota((big_total, LANES), 0) - base, marks, 0.0)

    my_row = nt(jnp.ones((8, LANES), BF16), big_marks[0:group, :].astype(BF16))[0:1]
    best = jnp.full((1, group), -1.0, F32)
    for r in range(shards):
        if r:
            two_copy(r).wait_recv()
            if r % cores == 0 and cores > 1:
                two_copy(r + 1).start()
        theirs = pl.ds(r * group, group)
        scores = nt(big_all[theirs, :], big_all[0:group, :])
        allowed = jnp.sum(big_marks[theirs, :], axis=1, keepdims=True) == my_row
        if r == 0:
            allowed = allowed & (iota((group, group), 0) != iota((group, group), 1))
        best = jnp.maximum(best, jnp.max(jnp.where(allowed, scores, -1.0), axis=0, keepdims=True))
    big_back[:, 0:group] = best
    for j in away:
        bback_copy(j).start()
    back_recv[n] = big_back[:, window(0, cb)]

    def small_best(r0, r1, c0, c1):
        scores = nt(small_recv[r0:r1, :], small_recv[c0:c1, :])
        allowed = small_col[r0:r1] == small_row[:, c0:c1]
        if r0 < c1 and c0 < r1:
            allowed = allowed & (iota((r1 - r0, c1 - c0), 0) + r0 != iota((r1 - r0, c1 - c0), 1) + c0)
        return jnp.max(jnp.where(allowed, scores, -1.0), axis=0, keepdims=True)

    last = [(shards - 1, j) for j in range(blocks)]
    arrivals = [(r, j) for r in range(shards) for j in range(blocks) if (r, j) != (0, 0)]
    if tight:
        for r in range(1, shards):
            for j in far:
                if r % cores or r + 1 == shards or cores == 1:
                    over_copy(r, j).wait_recv()
    for r, j in arrivals:
        if (r, j) not in last:
            (line_copy if j else side_copy)(r, j).wait_recv()
    cut = total - span
    edge = cut // LANES * LANES
    width = next(w for w in (256, 128) if edge % w == 0)
    for c in range(0, edge, width):
        small_back[:, c : c + width] = small_best(0, cut, c, c + width)
    if tight:
        for s in others:
            flag_copy(s).wait_recv()
            flag_copy(s).wait_send()
        flag_ref[...] = jnp.max(flags[:, 0, :], axis=0, keepdims=True)
    else:
        flag_ref[...] = jnp.zeros_like(flag_ref)
    for j in away:
        one_copy(j).wait_send()
    for r in range(1, shards):
        two_copy(r).wait_send()
    for q, r, j in peers:
        ids_copy(q, r, j).wait_send()
        if r:
            side_copy(r, j).wait_send()
        if j and (r, j) not in last:
            line_copy(r, j).wait_send()
    if tight:
        for j, i in [(half, None)] + hops:
            bover_copy(j, i).wait_send()
            for r in range(1, shards):
                over_copy(r, j).wait_send()
    for r, j in last:
        (line_copy if j else side_copy)(r, j).wait_recv()
    for c in range(0, edge, edge):
        small_back[:, 0:edge] = jnp.maximum(small_back[:, 0:edge], small_best(cut, total, 0, edge))
    early = [p for p in peers if p[0] * cs // LANES * LANES + 2 * LANES <= edge]
    for q, r, j in early:
        sback_copy(q, r, j).start()
    small_back[:, edge:total] = small_best(0, total, edge, total)
    for q, r, j in peers:
        if (q, r, j) not in early:
            sback_copy(q, r, j).start()
    back_recv[0] = small_back[:, window(0, cs)]

    for j in away:
        bback_copy(j).wait_recv()
    for q, r, j in peers:
        sback_copy(q, r, j).wait_recv()
    result = exact_dot(back_recv[:, 0, :], at_lane[...])
    out_ref[...] = jnp.sum(jnp.where(onehot, result, 0.0), axis=0, keepdims=True)

    for j in away:
        bback_copy(j).wait_send()
    for q, r, j in peers:
        sback_copy(q, r, j).wait_send()
    for r, j in last:
        if j:
            line_copy(r, j).wait_send()


def solution(mesh):
    slabs, shards, blocks = mesh.shape["slab"], mesh.shape["docs"], mesh.shape["blk"]
    n = shards * blocks

    def body(pooled, proj_weight, cluster):
        rows, width = pooled.shape
        feature = proj_weight.shape[1]
        big_count = rows // 4
        cap_big = 2 * big_count // shards
        cap_small = 2 * (rows - big_count) // n
        cs = up(cap_small, 16)
        cb = up(cap_big * (shards // blocks), 16)
        nb = up(n + blocks, 16)
        dma = pltpu.SemaphoreType.DMA

        def call(ms, mb, collective_id):
            return pl.pallas_call(
                functools.partial(kernel, (slabs, shards, blocks, cs, ms, cb, mb)),
                out_shape=(jax.ShapeDtypeStruct((1, rows), F32), jax.ShapeDtypeStruct((1, LANES), F32)),
                in_specs=[
                    pl.BlockSpec(memory_space=pl.ANY),
                    pl.BlockSpec(memory_space=pl.ANY),
                    pl.BlockSpec(memory_space=pltpu.VMEM),
                ],
                out_specs=(pl.BlockSpec(memory_space=pltpu.VMEM), pl.BlockSpec(memory_space=pltpu.VMEM)),
                scratch_shapes=[
                    pltpu.VMEM((rows, width), BF16),
                    pltpu.VMEM((width, feature), BF16),
                    pltpu.VMEM((rows, feature), BF16),
                    pltpu.VMEM((n * cs, feature), BF16),
                    pltpu.VMEM((n * cs, feature), BF16),
                    pltpu.VMEM((n * cs, feature), BF16),
                    pltpu.VMEM((blocks * cb, feature), BF16),
                    pltpu.VMEM((n * cb, feature), BF16),
                    pltpu.VMEM((max(cb - mb, 16), feature), BF16),
                    pltpu.VMEM((n, 1, 2 * LANES), F32),
                    pltpu.VMEM((n, 1, 2 * LANES), F32),
                    pltpu.VMEM((slabs, 1, LANES), F32),
                    pltpu.VMEM((n * cb, LANES), F32),
                    pltpu.VMEM((1, up(n * cs, LANES) + LANES), F32),
                    pltpu.VMEM((1, up(blocks * cb, LANES) + LANES), F32),
                    pltpu.VMEM((nb, 1, 2 * LANES), F32),
                    pltpu.VMEM((2 * LANES, rows), BF16),
                    dma((2,)), dma((n,)), dma((n,)), dma((n,)), dma((n,)), dma((n,)), dma((n,)),
                    dma((blocks,)), dma((blocks,)), dma((shards,)), dma((shards,)), dma((n,)), dma((n,)),
                    dma((blocks,)), dma((blocks,)), dma((n,)), dma((n,)),
                    dma((blocks,)), dma((blocks,)), dma((slabs,)), dma((slabs,)), pltpu.SemaphoreType.REGULAR,
                ],
                compiler_params=pltpu.CompilerParams(
                    collective_id=collective_id, has_side_effects=True, vmem_limit_bytes=60 * 1024 * 1024
                ),
            )(pooled, proj_weight, cluster.reshape(1, rows))

        ms, mb = up(2 * cs // 3, 16), up(cb // 2, 16)
        if ms < cs and mb < cb and cs - ms <= cb - mb:
            best, flag = call(ms, mb, 0)
            best = lax.cond(flag[0, 0] > 0.0, lambda: call(cs, cb, 1)[0], lambda: best)
        else:
            best, _ = call(cs, cb, 0)
        return jnp.maximum(best.reshape(rows), -1.0)

    in_specs = (P(("slab", "docs", "blk"), None), P(), P(("slab", "docs", "blk")))
    out_specs = P(("slab", "docs", "blk"))
    return jax.shard_map(body, mesh=mesh, in_specs=in_specs, out_specs=out_specs, check_vma=False)
```
